32 devices in a mesh: grp: 2 (over x), ctx: 8 (over z, y), head: 2 (over core).
Axes of the slice: x: 2, y: 2, z: 4, core: 2. Of those that a mesh axis runs over, the one named last changes fastest.
Arguments:
- cache_keys: bfloat16 [16, 8, 2048, 128], P('grp', 'head', 'ctx'), parts along dimension 0, may hold values from -4 to 4
- cache_values: bfloat16 [16, 8, 2048, 128], P('grp', 'head', 'ctx'), parts along dimension 0, may hold values from -8 to 8
- ref_queries: bfloat16 [16, 8, 256, 128], P('grp', 'head'), parts along dimension 0, may hold values from -264 to 264
- listed: int32 [16, 8, 128], P('grp', 'head'), parts along dimension 0, may hold values from 0 to 2047, as said below
Outputs:
- compact_keys: bfloat16 [16, 8, 128, 128], P('grp', 'head'), parts along dimension 0
- compact_values: bfloat16 [16, 8, 128, 128], P('grp', 'head'), parts along dimension 0
The draws below stay inside these ranges and needn't reach their ends.
There are 2 independent parts, one for each index of `grp`. The reference program is written for one: setup_inputs(seed, part) draws one part's arguments, and reference() takes and returns one part's arrays. A program takes and returns all parts, laid end to end along the dimension named above; each array names one. Nothing has to cross between parts.
Inputs may be any that keep to these rules, and one draw needn't show every extreme that they name: `listed`: for each layer and head the 128 positions are distinct; at most 16 of them lie in one aligned block of 256 positions, and exactly 16 in some block.
All inputs are finite; a program needn't handle non-finite values.
Results may differ from the reference program's by a relative error of at most 0.0046.
Values may be sent and summed in bfloat16 or wider, within the bound.
No kernel may reach another device: no remote copies, remote signals or barrier semaphores. Data moves between devices by JAX's collectives and lax.ppermute only.
A program may use at most 64 MiB of HBM per device.

```python
import math
import jax
import jax.numpy as jnp
from jax import lax

HD = 128
KV_HEADS = 8
LAYERS = 8
TOK_DEV = 256
NQ = 256
KEEP = 128
CAP = 16
SLAB = 2048


def listed_positions(key):
    base = jax.random.fold_in(key, 7)
    shard_count = SLAB // TOK_DEV
    count = LAYERS * KV_HEADS
    key_one, key_two, key_three, key_four = jax.random.split(base, 4)
    order_scores = jax.random.randint(key_one, (count, shard_count, TOK_DEV), 0, 2 ** 20) * TOK_DEV
    order_scores = order_scores + jnp.arange(TOK_DEV, dtype=jnp.int32)[None, None, :]
    offsets = jnp.argsort(order_scores, axis=-1)[:, :, :CAP].astype(jnp.int32)
    shard_bias = jax.random.randint(key_two, (count, shard_count), 0, 4)
    hottest = jax.random.randint(key_three, (count,), 0, shard_count)
    shard_bias = jnp.where(jnp.arange(shard_count)[None, :] == hottest[:, None], 4, shard_bias)
    noise = jax.random.randint(key_four, (count, shard_count, CAP), 0, 2 ** 16)
    flat_index = jnp.arange(shard_count * CAP, dtype=jnp.int32).reshape(1, shard_count, CAP)
    ranked = shard_bias[:, :, None] * 2 ** 22 + noise * (shard_count * CAP) + flat_index
    chosen = lax.top_k(ranked.reshape(count, shard_count * CAP), KEEP)[1].astype(jnp.int32)
    home_shard = chosen // CAP
    within = jnp.take_along_axis(offsets.reshape(count, shard_count * CAP), chosen, axis=1)
    return (home_shard * TOK_DEV + within).reshape(LAYERS, KV_HEADS, KEEP).astype(jnp.int32)


def drawn_pair(key):
    base = jax.random.fold_in(key, 5)
    key_one, key_two = jax.random.split(base, 2)
    shape = (LAYERS, KV_HEADS, SLAB, HD)
    key_table = jax.random.truncated_normal(key_one, -4.0, 4.0, shape, jnp.float32)
    queries = 1.5 * jax.random.truncated_normal(key_two, -4.0, 4.0, (LAYERS, KV_HEADS, NQ, HD), jnp.float32)
    return (key_table, queries)


def draw_cache_keys(key, part):
    return drawn_pair(key)[0].astype(jnp.bfloat16)


def draw_ref_queries(key, part):
    return drawn_pair(key)[1].astype(jnp.bfloat16)


def draw_listed(key, part):
    return listed_positions(key)


def levels(rng, dims, shards, smallest, largest):
    loudness = 1.0
    for dim, parts in shards:
        steps = jax.random.uniform(jax.random.fold_in(jax.random.fold_in(rng, 6), dim), (parts,), jnp.float32, smallest / len(shards), largest / len(shards))
        loudness = loudness * jnp.repeat(jnp.exp(steps), dims[dim] // parts).reshape((-1,) + (1,) * (len(dims) - 1 - dim))
    return loudness


def scatter_about(rng, shape, deviation, most, shards=(), held_as=jnp.bfloat16):
    values = jax.random.normal(rng, shape, jnp.float32) * deviation
    if len(shards) > 0:
        values = levels(rng, shape, shards, -0.22, 0.18) * values
    return jnp.clip(values, min=-most, max=most).astype(held_as)


def setup_inputs(seed: int = 0, part: int = 0) -> dict:
    keys = jax.random.split(jax.random.key(seed), 5)
    own_keys = jax.random.split(jax.random.fold_in(keys[4], part), 5)
    return {
        "cache_keys": draw_cache_keys(jax.random.fold_in(jax.random.fold_in(keys[4], part), 71), part),
        "cache_values": scatter_about(own_keys[1], (LAYERS, KV_HEADS, SLAB, HD), 2.0, 8.0, ((1, 2), (2, 8))),
        "ref_queries": draw_ref_queries(jax.random.fold_in(jax.random.fold_in(keys[4], part), 71), part),
        "listed": draw_listed(jax.random.fold_in(jax.random.fold_in(keys[4], part), 71), part),
    }


ridge_share = 0.05

def fit_one(pieces):
    queries, key_table, value_table, positions = pieces
    score_scale = 1.0 / math.sqrt(HD)
    scores = jnp.dot(queries.astype(jnp.float32), key_table.T.astype(jnp.float32), preferred_element_type=jnp.float32) * score_scale
    row_peak = lax.optimization_barrier(jnp.max(scores, axis=-1, keepdims=True))
    expw = jnp.exp(scores - row_peak)
    totals = lax.optimization_barrier(jnp.sum(expw, axis=-1))
    weighted = jnp.dot(expw.astype(jnp.bfloat16).astype(jnp.float32), value_table.astype(jnp.float32), preferred_element_type=jnp.float32)
    target = weighted / totals[:, None]
    picked = jnp.take(key_table, positions.astype(jnp.int32), axis=0)
    compact_scores = jnp.dot(queries.astype(jnp.float32), picked.T.astype(jnp.float32), preferred_element_type=jnp.float32) * score_scale
    fit_weights = jax.nn.softmax(compact_scores, axis=-1)
    gram_matrix = jnp.dot(fit_weights.T, fit_weights, precision=lax.Precision.HIGHEST)
    moments = jnp.dot(fit_weights.T, target, precision=lax.Precision.HIGHEST)
    ridge_term = ridge_share * jnp.trace(gram_matrix) / KEEP
    system = gram_matrix + ridge_term * jnp.eye(KEEP, dtype=jnp.float32)
    factor = jnp.linalg.cholesky(system)
    halfway = lax.linalg.triangular_solve(factor, moments, left_side=True, lower=True)
    solved = lax.linalg.triangular_solve(factor, halfway, left_side=True, lower=True, transpose_a=True)
    return (picked, solved.astype(jnp.bfloat16))

def reference(cache_keys, cache_values, ref_queries, listed):
    count = LAYERS * KV_HEADS
    query_rows = ref_queries.reshape(count, NQ, HD)
    key_rows = cache_keys.reshape(count, SLAB, HD)
    value_rows = cache_values.reshape(count, SLAB, HD)
    positions = listed.reshape(count, KEEP)
    picked, solved = lax.map(fit_one, (query_rows, key_rows, value_rows, positions))
    return (picked.reshape(LAYERS, KV_HEADS, KEEP, HD), solved.reshape(LAYERS, KV_HEADS, KEEP, HD))
```

```python
import functools
import math

import jax
import jax.numpy as jnp
from jax import lax
from jax.experimental import pallas as pl
from jax.experimental.pallas import tpu as pltpu
from jax.sharding import PartitionSpec as P


ridge_share = 0.05
CAP = 16
STAT_ROWS = 16
F32 = jnp.float32
BF16 = jnp.bfloat16
HIGHEST = lax.Precision.HIGHEST


def contract(a, b, dim_a, dim_b, precision=None):
    return lax.dot_general(
        a, b, (((dim_a,), (dim_b,)), ((), ())), precision=precision, preferred_element_type=F32
    )


def iota(shape, dim):
    return lax.broadcasted_iota(jnp.int32, shape, dim)


def rows_kernel(local_ref, keys_ref, rows_ref, *, cap):
    items, tok, _ = keys_ref.shape
    keep = local_ref.shape[2]
    local = local_ref[:, 0, :]
    mine = ((local >= 0) & (local < tok)).astype(F32)
    before = (iota((keep, keep), 0) < iota((keep, keep), 1)).astype(F32)
    rank = jnp.dot(mine, before, preferred_element_type=F32)
    rank = jnp.where(mine > 0, rank, -1.0)
    local = local.astype(F32)
    for i in range(items):
        chosen = iota((cap, keep), 0).astype(F32) == rank[i : i + 1]
        where_at = jnp.sum(jnp.where(chosen, local[i : i + 1] + 1.0, 0.0), axis=1, keepdims=True)
        pick = (iota((cap, tok), 1).astype(F32) + 1.0 == where_at).astype(BF16)
        rows_ref[i] = jnp.dot(pick, keys_ref[i], preferred_element_type=F32).astype(BF16)


def listed_rows(local, key_table, cap):
    items, tok, hd = key_table.shape
    keep = local.shape[1]
    step = 8 if items % 8 == 0 else 1
    return pl.pallas_call(
        functools.partial(rows_kernel, cap=cap),
        grid=(items // step,),
        in_specs=[
            pl.BlockSpec((step, 1, keep), lambda i: (i, 0, 0)),
            pl.BlockSpec((step, tok, hd), lambda i: (i, 0, 0)),
        ],
        out_specs=pl.BlockSpec((step, cap, hd), lambda i: (i, 0, 0)),
        out_shape=jax.ShapeDtypeStruct((items, cap, hd), BF16),
        name="listed_rows",
    )(local[:, None, :], key_table)


def split_rows(total):
    high = total.astype(BF16).astype(F32)
    return high, total - high


def row_of(table, index):
    picked = jnp.where(iota(table.shape, 0) == index, table, 0.0)
    return jnp.sum(picked, axis=0, keepdims=True)


def partial_kernel(owner_ref, q_ref, k_ref, v_ref, *refs, scale, merge):
    if merge:
        other_ref, out_ref, stat_ref = refs
    else:
        out_ref, stat_ref = refs
    i = pl.program_id(0)
    hd = q_ref.shape[2]
    nq = q_ref.shape[1]
    item_rows = out_ref.shape[0] - STAT_ROWS
    scores = contract(k_ref[0], q_ref[0], 1, 1) * scale
    peak = jnp.max(scores, axis=0, keepdims=True).astype(BF16).astype(F32)
    expw = jnp.exp(scores - peak)
    total = jnp.sum(expw, axis=0, keepdims=True)
    weighted = contract(v_ref[0], expw.astype(BF16), 0, 0)
    at = pl.multiple_of(i * hd, hd)
    if merge:
        other = other_ref[pl.ds(item_rows, STAT_ROWS), :].astype(F32)
        other_peak = row_of(other, 3 * i)
        other_total = row_of(other, 3 * i + 1) + row_of(other, 3 * i + 2)
        both = jnp.maximum(peak, other_peak)
        here, there = jnp.exp(peak - both), jnp.exp(other_peak - both)
        total = total * here + other_total * there
        weighted = weighted * here + other_ref[pl.ds(at, hd), :].astype(F32) * there
        peak = both
    out_ref[pl.ds(at, hd), :] = weighted.astype(BF16)
    high, low = split_rows(total)
    row = iota((STAT_ROWS, nq), 0)
    stats = jnp.where(i == 0, jnp.zeros_like(stat_ref), stat_ref[...])
    stats = jnp.where(row == 3 * i, peak, stats)
    stats = jnp.where(row == 3 * i + 1, high, stats)
    stats = jnp.where(row == 3 * i + 2, low, stats)
    stat_ref[...] = stats
    out_ref[pl.ds(item_rows, STAT_ROWS), :] = stats.astype(BF16)


def partial_attention(owner, items, queries, key_table, value_table, scale, other=None):
    _, tok, hd = key_table.shape
    nq = queries.shape[1]
    shape = (items * hd + STAT_ROWS, nq)

    def block(i, owner_ref):
        return (owner_ref[0] * items + i, 0, 0)

    whole = pl.BlockSpec(shape, lambda i, owner_ref: (0, 0))
    specs = [
        pl.BlockSpec((1, nq, hd), block),
        pl.BlockSpec((1, tok, hd), block),
        pl.BlockSpec((1, tok, hd), block),
    ]
    operands = [queries, key_table, value_table]
    if other is not None:
        specs.append(whole)
        operands.append(other)
    return pl.pallas_call(
        functools.partial(partial_kernel, scale=scale, merge=other is not None),
        grid_spec=pltpu.PrefetchScalarGridSpec(
            num_scalar_prefetch=1,
            grid=(items,),
            in_specs=specs,
            out_specs=whole,
            scratch_shapes=[pltpu.VMEM((STAT_ROWS, nq), F32)],
        ),
        out_shape=jax.ShapeDtypeStruct(shape, BF16),
        name="partial_merge" if other is not None else "partial_attention",
    )(owner[None], *operands)


def in_listed_order(slots, pieces):
    table = jnp.concatenate(pieces, axis=0)
    pick = (iota((table.shape[0], slots.shape[1]), 0) == slots).astype(BF16)
    return contract(pick, table, 0, 0).astype(BF16)


def order_kernel(slots_ref, *refs):
    pieces, out_ref = refs[:-1], refs[-1]
    for i in range(out_ref.shape[0]):
        out_ref[i] = in_listed_order(slots_ref[i], [piece[i] for piece in pieces])


def order_rows(slots, pieces):
    items, cap, hd = pieces[0].shape
    keep = slots.shape[1]
    step = 8 if items % 8 == 0 else 1
    return pl.pallas_call(
        order_kernel,
        grid=(items // step,),
        in_specs=[pl.BlockSpec((step, 1, keep), lambda i: (i, 0, 0))]
        + [pl.BlockSpec((step, cap, hd), lambda i: (i, 0, 0))] * len(pieces),
        out_specs=pl.BlockSpec((step, keep, hd), lambda i: (i, 0, 0)),
        out_shape=jax.ShapeDtypeStruct((items, keep, hd), BF16),
        name="order_rows",
    )(slots[:, None, :], *pieces)


def system_kernel(owner_ref, slots_ref, q_ref, *refs, scale):
    pieces, (weights_ref, inverse_ref) = refs[:-2], refs[-2:]
    items, keep, nq = weights_ref.shape
    eye = iota((keep, keep), 0) == iota((keep, keep), 1)
    for i in range(items):
        compact = in_listed_order(slots_ref[i], [piece[i] for piece in pieces])
        scores = contract(compact, q_ref[i], 1, 1) * scale
        expw = jnp.exp(scores - jnp.max(scores, axis=0, keepdims=True))
        weights = expw / jnp.sum(expw, axis=0, keepdims=True)
        weights_ref[i] = weights
        gram = contract(weights, weights, 1, 1, HIGHEST)
        ridge = ridge_share * jnp.sum(jnp.where(eye, gram, 0.0)) / keep
        inverse_ref[i] = gram + jnp.where(eye, ridge, 0.0)
    lane = iota((1, keep), 1)
    wide_lane = iota((keep, keep), 1)

    def sweep(k, carry):
        at = jnp.full((keep, keep), k, jnp.int32)
        for i in range(items):
            table = inverse_ref[i]
            row = inverse_ref[i, pl.ds(k, 1), :]
            column = jnp.take_along_axis(table, at, axis=1)
            pivot = 1.0 / jnp.sum(jnp.where(lane == k, row, 0.0), axis=1, keepdims=True)
            scaled = row * pivot
            inverse_ref[i] = jnp.where(wide_lane == k, column * pivot, table - column * scaled)
            inverse_ref[i, pl.ds(k, 1), :] = jnp.where(lane == k, -pivot, scaled)
        return carry

    lax.fori_loop(0, keep, sweep, 0)


def ridge_system(owner, items, slots, queries, pieces, scale):
    _, cap, hd = pieces[0].shape
    keep = slots.shape[1]
    nq = queries.shape[1]

    def block(i, owner_ref):
        return (owner_ref[0], 0, 0)

    def whole(i, owner_ref):
        return (0, 0, 0)

    return pl.pallas_call(
        functools.partial(system_kernel, scale=scale),
        grid_spec=pltpu.PrefetchScalarGridSpec(
            num_scalar_prefetch=1,
            grid=(1,),
            in_specs=[
                pl.BlockSpec((items, 1, keep), block),
                pl.BlockSpec((items, nq, hd), block),
            ]
            + [pl.BlockSpec((items, cap, hd), block)] * len(pieces),
            out_specs=[
                pl.BlockSpec((items, keep, nq), whole),
                pl.BlockSpec((items, keep, keep), whole),
            ],
        ),
        out_shape=[
            jax.ShapeDtypeStruct((items, keep, nq), F32),
            jax.ShapeDtypeStruct((items, keep, keep), F32),
        ],
        name="ridge_system",
    )(owner[None], slots[:, None, :], queries, *pieces)


def solve_kernel(weights_ref, inverse_ref, *refs):
    parts, out_ref = refs[:-1], refs[-1]
    items, _, hd = out_ref.shape
    stats = [part[pl.ds(items * hd, STAT_ROWS), :].astype(F32) for part in parts]
    for i in range(items):
        peaks = [stat[3 * i : 3 * i + 1] for stat in stats]
        top = functools.reduce(jnp.maximum, peaks)
        total, weighted = 0.0, 0.0
        for part, stat, peak in zip(parts, stats, peaks):
            share = jnp.exp(peak - top)
            total = total + share * (stat[3 * i + 1 : 3 * i + 2] + stat[3 * i + 2 : 3 * i + 3])
            weighted = weighted + share * part[pl.ds(i * hd, hd), :].astype(F32)
        target = weighted / total
        moments = contract(weights_ref[i], target, 1, 1, HIGHEST)
        out_ref[i] = -contract(inverse_ref[i], moments, 1, 0, HIGHEST).astype(BF16)


def solve_items(weights, inverse, parts):
    items, keep, _ = weights.shape
    hd = (parts[0].shape[0] - STAT_ROWS) // items

    return pl.pallas_call(
        solve_kernel,
        out_shape=jax.ShapeDtypeStruct((items, keep, hd), BF16),
        name="solve_items",
    )(weights, inverse, *parts)


def place_kernel(me_ref, *refs):
    pieces, out_ref, sems = refs[:-2], refs[-2], refs[-1]
    items = pieces[0].shape[0]
    copies = []
    for d, piece in enumerate(pieces):
        at = (me_ref[0] ^ d) * items
        copies.append(pltpu.make_async_copy(piece, out_ref.at[pl.ds(at, items)], sems.at[d]))
    for copy in copies:
        copy.start()
    for copy in copies:
        copy.wait()


def place_blocks(me, pieces):
    items, keep, hd = pieces[0].shape
    return pl.pallas_call(
        place_kernel,
        grid_spec=pltpu.PrefetchScalarGridSpec(
            num_scalar_prefetch=1,
            grid=(1,),
            in_specs=[pl.BlockSpec(memory_space=pl.ANY)] * len(pieces),
            out_specs=pl.BlockSpec(memory_space=pl.ANY),
            scratch_shapes=[pltpu.SemaphoreType.DMA((len(pieces),))],
        ),
        out_shape=jax.ShapeDtypeStruct((items * len(pieces), keep, hd), BF16),
        name="place_blocks",
    )(me[None], *pieces)


def gather_blocks(block, swap, shard_count):
    pieces = {0: block}
    for d in range(2, shard_count, 2):
        pieces[d] = swap(block, d)
    for d in range(0, shard_count, 2):
        pieces[d + 1] = swap(pieces[d], 1)
    return [pieces[d] for d in range(shard_count)]


def shards(cache_keys, cache_values, ref_queries, listed):
    layer_count, head_count, tok_local, head_size = cache_keys.shape
    query_count = ref_queries.shape[2]
    keep_count = listed.shape[2]
    item_count = layer_count * head_count
    shard_count = lax.axis_size("ctx")
    items_local = item_count // shard_count
    me = lax.axis_index("ctx").astype(jnp.int32)
    scale = 1.0 / math.sqrt(head_size)
    cap = min(CAP, tok_local, keep_count)
    queries = ref_queries.reshape(item_count, query_count, head_size)
    key_table = cache_keys.reshape(item_count, tok_local, head_size)
    value_table = cache_values.reshape(item_count, tok_local, head_size)
    positions = listed.reshape(item_count, keep_count)

    def swap(x, d):
        return lax.ppermute(x, "ctx", [(j, j ^ d) for j in range(shard_count)])

    rows = listed_rows(positions - me * tok_local, key_table, cap)
    pieces = gather_blocks(rows, swap, shard_count)

    order = list(range(2, shard_count, 2)) + [0]
    sent = [
        swap(partial_attention(me ^ (d + 1), items_local, queries, key_table, value_table, scale), 1)
        for d in order
    ]
    parts = []
    for d, other in zip(order, sent):
        merged = partial_attention(
            me ^ d, items_local, queries, key_table, value_table, scale, other
        )
        parts.append(swap(merged, d) if d else merged)

    home = positions // tok_local
    earlier = jnp.arange(keep_count)[:, None] < jnp.arange(keep_count)[None, :]
    same = (home[:, :, None] == home[:, None, :]) & earlier[None]
    slots = (home ^ me) * cap + jnp.sum(same.astype(jnp.int32), axis=1)

    weights, inverse = ridge_system(me, items_local, slots, queries, pieces, scale)
    solved = solve_items(weights, inverse, parts)
    compact_keys = order_rows(slots, pieces)
    compact_values = place_blocks(me, gather_blocks(solved, swap, shard_count))
    shape = (layer_count, head_count, keep_count, head_size)
    return (compact_keys.reshape(shape), compact_values.reshape(shape))


def solution(mesh):
    in_specs = (
        P("grp", "head", "ctx", None),
        P("grp", "head", "ctx", None),
        P("grp", "head", None, None),
        P("grp", "head", None),
    )
    out_specs = (P("grp", "head", None, None), P("grp", "head", None, None))
    return jax.shard_map(shards, mesh=mesh, in_specs=in_specs, out_specs=out_specs, check_vma=False)
```

```python
import functools
import math

import jax
import jax.numpy as jnp
from jax import lax
from jax.experimental import pallas as pl
from jax.experimental.pallas import tpu as pltpu
from jax.sharding import PartitionSpec as P


ridge_share = 0.05
CAP = 16
STAT_ROWS = 16
BLOCK = 32
TILE = 8
F32 = jnp.float32
BF16 = jnp.bfloat16
HIGHEST = lax.Precision.HIGHEST


def contract(a, b, dim_a, dim_b, precision=None):
    return lax.dot_general(
        a, b, (((dim_a,), (dim_b,)), ((), ())), precision=precision, preferred_element_type=F32
    )


def iota(shape, dim):
    return lax.broadcasted_iota(jnp.int32, shape, dim)


def rows_kernel(local_ref, keys_ref, rows_ref, keys_buf, sems):
    items, tok, _ = keys_ref.shape
    _, cap, _ = rows_ref.shape
    keep = local_ref.shape[1]
    chunks = sems.shape[0]
    size = items // chunks
    copies = [
        pltpu.make_async_copy(
            keys_ref.at[pl.ds(c * size, size)], keys_buf.at[pl.ds(c * size, size)], sems.at[c]
        )
        for c in range(chunks)
    ]
    for copy in copies:
        copy.start()
    local = local_ref[...]
    mine = ((local >= 0) & (local < tok)).astype(F32)
    before = (iota((keep, keep), 0) < iota((keep, keep), 1)).astype(F32)
    rank = jnp.dot(mine, before, preferred_element_type=F32)
    rank = jnp.where(mine > 0, rank, -1.0)
    local = local.astype(F32)
    for i in range(items):
        if i % size == 0:
            copies[i // size].wait()
        chosen = iota((cap, keep), 0).astype(F32) == rank[i : i + 1]
        where_at = jnp.sum(jnp.where(chosen, local[i : i + 1] + 1.0, 0.0), axis=1, keepdims=True)
        pick = (iota((cap, tok), 1).astype(F32) + 1.0 == where_at).astype(BF16)
        rows_ref[i] = jnp.dot(pick, keys_buf[i], preferred_element_type=F32).astype(BF16)


def listed_rows(local, key_table, cap):
    items, tok, hd = key_table.shape
    chunks = 4 if items % 4 == 0 else 1
    return pl.pallas_call(
        rows_kernel,
        in_specs=[pl.BlockSpec(memory_space=pltpu.VMEM), pl.BlockSpec(memory_space=pl.ANY)],
        out_shape=jax.ShapeDtypeStruct((items, cap, hd), BF16),
        scratch_shapes=[
            pltpu.VMEM((items, tok, hd), BF16),
            pltpu.SemaphoreType.DMA((chunks,)),
        ],
        name="listed_rows",
    )(local, key_table)


def stat_table(peaks, totals):
    rows = []
    for peak, total in zip(peaks, totals):
        high = total.astype(BF16).astype(F32)
        rows += [peak, high, total - high]
    row = iota((STAT_ROWS, peaks[0].shape[1]), 0)
    table = jnp.zeros(row.shape, F32)
    for r, value in enumerate(rows):
        table = jnp.where(row == r, value, table)
    return table


def stats_of(table, i):
    return table[3 * i : 3 * i + 1], table[3 * i + 1 : 3 * i + 2] + table[3 * i + 2 : 3 * i + 3]


def message_rows(items, hd):
    return items * hd + STAT_ROWS


def partial_kernel(me_ref, q_ref, k_ref, v_ref, *refs, moves, scale, after):
    out_ref, q_buf, k_buf, v_buf, sems = refs[after:]
    _, items, _, hd = q_buf.shape
    rows = message_rows(items, hd)
    copies = []
    for j, move in enumerate(moves):
        at = pl.ds((me_ref[0] ^ move) * items, items)
        trio = ((q_ref, q_buf), (k_ref, k_buf), (v_ref, v_buf))
        copies.append(
            [
                pltpu.make_async_copy(source.at[at], buf.at[j], sems.at[j, n])
                for n, (source, buf) in enumerate(trio)
            ]
        )
    for group in copies:
        for copy in group:
            copy.start()

    def score(j, i):
        if i == 0:
            for copy in copies[j]:
                copy.wait()
        return contract(k_buf[j, i], q_buf[j, i], 1, 1)

    steps = [(j, i) for j in range(len(moves)) for i in range(items)]
    upcoming = score(*steps[0])
    for n, (j, i) in enumerate(steps):
        scores = upcoming
        if n + 1 < len(steps):
            upcoming = score(*steps[n + 1])
        if i == 0:
            peaks, totals = [], []
        peak = (jnp.max(scores, axis=0, keepdims=True) * scale).astype(BF16).astype(F32)
        expw = jnp.exp2(scores * scale - peak)
        peaks.append(peak)
        totals.append(jnp.sum(expw, axis=0, keepdims=True))
        weighted = contract(v_buf[j, i], expw.astype(BF16), 0, 0)
        out_ref[pl.ds(j * rows + i * hd, hd), :] = weighted.astype(out_ref.dtype)
        if i == items - 1:
            table = stat_table(peaks, totals)
            out_ref[pl.ds(j * rows + items * hd, STAT_ROWS), :] = table.astype(out_ref.dtype)


def partial_attention(me, moves, items, queries, key_table, value_table, scale, dtype, after=()):
    _, tok, hd = key_table.shape
    nq = queries.shape[1]
    shape = (len(moves) * message_rows(items, hd), nq)
    anywhere = pl.BlockSpec(memory_space=pl.ANY)
    return pl.pallas_call(
        functools.partial(
            partial_kernel, moves=moves, scale=scale * math.log2(math.e), after=len(after)
        ),
        grid_spec=pltpu.PrefetchScalarGridSpec(
            num_scalar_prefetch=1,
            grid=(1,),
            in_specs=[anywhere] * (3 + len(after)),
            out_specs=pl.BlockSpec(shape, lambda i, me_ref: (0, 0)),
            scratch_shapes=[
                pltpu.VMEM((len(moves), items, nq, hd), BF16),
                pltpu.VMEM((len(moves), items, tok, hd), BF16),
                pltpu.VMEM((len(moves), items, tok, hd), BF16),
                pltpu.SemaphoreType.DMA((len(moves), 3)),
            ],
        ),
        out_shape=jax.ShapeDtypeStruct(shape, dtype),
        name="partial_attention",
    )(me, queries, key_table, value_table, *after)


def merged_item(tables, parts, i, hd):
    stats = [stats_of(table, i) for table in tables]
    top = functools.reduce(jnp.maximum, [peak for peak, _ in stats])
    shares = [jnp.exp2(peak - top) for peak, _ in stats]
    total = sum(share * part_total for share, (_, part_total) in zip(shares, stats))
    at = pl.ds(i * hd, hd)
    weighted = sum(share * part[at, :].astype(F32) for share, part in zip(shares, parts))
    return top, total, weighted


def merge_kernel(*refs, items, count):
    parts, out_ref = refs[:count], refs[-1]
    hd = (out_ref.shape[0] - STAT_ROWS) // items
    tables = [part[pl.ds(items * hd, STAT_ROWS), :].astype(F32) for part in parts]
    peaks, totals = [], []
    for i in range(items):
        top, total, weighted = merged_item(tables, parts, i, hd)
        peaks.append(top)
        totals.append(total)
        out_ref[pl.ds(i * hd, hd), :] = weighted.astype(BF16)
    out_ref[pl.ds(items * hd, STAT_ROWS), :] = stat_table(peaks, totals).astype(BF16)


def part_spec(place, rows, nq):
    return pl.BlockSpec((rows, nq), lambda i: (place, 0))


def merge_parts(parts, items, rows, after=()):
    nq = parts[0][0].shape[1]
    return pl.pallas_call(
        functools.partial(merge_kernel, items=items, count=len(parts)),
        grid=(1,),
        in_specs=[part_spec(place, rows, nq) for _, place in parts]
        + [pl.BlockSpec(memory_space=pl.ANY)] * len(after),
        out_specs=part_spec(0, rows, nq),
        out_shape=jax.ShapeDtypeStruct((rows, nq), BF16),
        name="merge_parts",
    )(*[array for array, _ in parts], *after)


def in_listed_order(slots, pieces):
    table = jnp.concatenate(pieces, axis=0)
    pick = (iota((table.shape[0], slots.shape[1]), 0) == slots).astype(BF16)
    return contract(pick, table, 0, 0).astype(BF16)


def order_kernel(slots_ref, *refs):
    pieces, out_ref = refs[:-1], refs[-1]
    for i in range(out_ref.shape[0]):
        out_ref[i] = in_listed_order(slots_ref[i], [piece[i] for piece in pieces])


def order_rows(slots, pieces, after=()):
    items, _, hd = pieces[0].shape
    keep = slots.shape[1]

    def body(*refs):
        order_kernel(*refs[: 1 + len(pieces)], refs[-1])

    return pl.pallas_call(
        body,
        in_specs=[pl.BlockSpec(memory_space=pltpu.VMEM)] * (1 + len(pieces))
        + [pl.BlockSpec(memory_space=pl.ANY)] * len(after),
        out_shape=jax.ShapeDtypeStruct((items, keep, hd), BF16),
        name="order_rows",
    )(slots[:, None, :], *pieces, *after)


def sweep_pair(tiles, home, row, at, first, second, sublane):
    left = [jnp.broadcast_to(tile[:, at : at + 1], tile.shape) for tile in tiles]
    right = [jnp.broadcast_to(tile[:, at + 1 : at + 2], tile.shape) for tile in tiles]
    upper, lower = tiles[home][row : row + 1], tiles[home][row + 1 : row + 2]
    a, b = left[home][row : row + 1], right[home][row : row + 1]
    c = right[home][row + 1 : row + 2]
    inverse = 1.0 / (a * c - b * b)
    a, b, c = c * inverse, b * inverse, a * inverse
    upper, lower = a * upper - b * lower, c * lower - b * upper
    upper = jnp.where(first, -a, jnp.where(second, b, upper))
    lower = jnp.where(second, -c, jnp.where(first, b, lower))
    cut_upper = jnp.where(first, 1.0 - a, upper)
    cut_lower = jnp.where(second, 1.0 - c, lower)
    swept = [t - x * cut_upper - y * cut_lower for t, x, y in zip(tiles, left, right)]
    swept[home] = jnp.where(
        sublane == row, upper, jnp.where(sublane == row + 1, lower, swept[home])
    )
    return swept


def system_kernel(owner_ref, slots_ref, q_ref, *refs, scale):
    pieces, (weights_ref, inverse_ref) = refs[:-2], refs[-2:]
    items, keep, nq = weights_ref.shape
    eye = iota((keep, keep), 0) == iota((keep, keep), 1)
    for i in range(items):
        compact = in_listed_order(slots_ref[i], [piece[i] for piece in pieces])
        scores = contract(compact, q_ref[i], 1, 1) * scale
        expw = jnp.exp(scores - jnp.max(scores, axis=0, keepdims=True))
        weights = expw / jnp.sum(expw, axis=0, keepdims=True)
        weights_ref[i] = weights
        gram = contract(weights, weights, 1, 1, HIGHEST)
        ridge = ridge_share * jnp.sum(jnp.where(eye, gram, 0.0)) / keep
        inverse_ref[i] = gram + jnp.where(eye, ridge, 0.0)
    edge = BLOCK if keep % BLOCK == 0 else keep
    lane = iota((1, keep), 1)
    sublane = iota((TILE, keep), 0)
    for start in range(0, keep, edge):
        span = slice(start, start + edge)
        panels = [inverse_ref[i, span, :] for i in range(items)]
        swept = [[panel[t : t + TILE] for t in range(0, edge, TILE)] for panel in panels]
        for k in range(0, edge, 2):
            home, row = divmod(k, TILE)
            first, second = lane == start + k, lane == start + k + 1
            for i in range(items):
                swept[i] = sweep_pair(swept[i], home, row, start + k, first, second, sublane)
        for i in range(items):
            solved = jnp.concatenate(swept[i], axis=0)
            inverse_ref[i] = inverse_ref[i] - contract(panels[i], solved, 0, 0, HIGHEST)
            inverse_ref[i, :, span] = solved.T
            inverse_ref[i, span, :] = solved


def ridge_system(owner, items, slots, queries, pieces, scale):
    _, cap, hd = pieces[0].shape
    keep = slots.shape[1]
    nq = queries.shape[1]

    def block(i, owner_ref):
        return (owner_ref[0], 0, 0)

    def whole(i, owner_ref):
        return (0, 0, 0)

    return pl.pallas_call(
        functools.partial(system_kernel, scale=scale),
        grid_spec=pltpu.PrefetchScalarGridSpec(
            num_scalar_prefetch=1,
            grid=(1,),
            in_specs=[
                pl.BlockSpec((items, 1, keep), block),
                pl.BlockSpec((items, nq, hd), block),
            ]
            + [pl.BlockSpec((items, cap, hd), block)] * len(pieces),
            out_specs=[
                pl.BlockSpec((items, keep, nq), whole),
                pl.BlockSpec((items, keep, keep), whole),
            ],
        ),
        out_shape=[
            jax.ShapeDtypeStruct((items, keep, nq), F32),
            jax.ShapeDtypeStruct((items, keep, keep), F32),
        ],
        name="ridge_system",
    )(owner, slots[:, None, :], queries, *pieces)


def solve_kernel(weights_ref, inverse_ref, *refs):
    parts, out_ref = refs[:-1], refs[-1]
    items, _, hd = out_ref.shape
    tables = [part[pl.ds(items * hd, STAT_ROWS), :].astype(F32) for part in parts]
    for i in range(items):
        _, total, weighted = merged_item(tables, parts, i, hd)
        moments = contract(weights_ref[i], weighted / total, 1, 1, HIGHEST)
        out_ref[i] = -contract(inverse_ref[i], moments, 1, 0, HIGHEST).astype(BF16)


def solve_items(weights, inverse, parts, rows):
    items, keep, nq = weights.shape
    hd = (rows - STAT_ROWS) // items

    def whole(i):
        return (0, 0, 0)

    return pl.pallas_call(
        solve_kernel,
        grid=(1,),
        in_specs=[
            pl.BlockSpec((items, keep, nq), whole),
            pl.BlockSpec((items, keep, keep), whole),
        ]
        + [part_spec(place, rows, nq) for _, place in parts],
        out_specs=pl.BlockSpec((items, keep, hd), whole),
        out_shape=jax.ShapeDtypeStruct((items, keep, hd), BF16),
        name="solve_items",
    )(weights, inverse, *[array for array, _ in parts])


def place_kernel(me_ref, *refs):
    pieces, out_ref, sems = refs[:-2], refs[-2], refs[-1]
    items = pieces[0].shape[0]
    copies = []
    for d, piece in enumerate(pieces):
        at = (me_ref[0] ^ d) * items
        copies.append(pltpu.make_async_copy(piece, out_ref.at[pl.ds(at, items)], sems.at[d]))
    for copy in copies:
        copy.start()
    for copy in copies:
        copy.wait()


def place_blocks(me, pieces):
    items, keep, hd = pieces[0].shape
    whole = pl.BlockSpec(pieces[0].shape, lambda i, me_ref: (0, 0, 0))
    return pl.pallas_call(
        place_kernel,
        grid_spec=pltpu.PrefetchScalarGridSpec(
            num_scalar_prefetch=1,
            grid=(1,),
            in_specs=[whole] * len(pieces),
            out_specs=pl.BlockSpec(memory_space=pl.ANY),
            scratch_shapes=[pltpu.SemaphoreType.DMA((len(pieces),))],
        ),
        out_shape=jax.ShapeDtypeStruct((items * len(pieces), keep, hd), BF16),
        name="place_blocks",
    )(me, *pieces)


def gather_blocks(block, swap, shard_count):
    pieces = {0: block}
    for d in range(2, shard_count, 2):
        pieces[d] = swap(block, d)
    for d in range(0, shard_count, 2):
        pieces[d + 1] = swap(pieces[d], 1)
    return [pieces[d] for d in range(shard_count)]


def shards(cache_keys, cache_values, ref_queries, listed):
    layer_count, head_count, tok_local, head_size = cache_keys.shape
    query_count = ref_queries.shape[2]
    keep_count = listed.shape[2]
    item_count = layer_count * head_count
    shard_count = lax.axis_size("ctx")
    items_local = item_count // shard_count
    me = lax.axis_index("ctx").astype(jnp.int32)
    scale = 1.0 / math.sqrt(head_size)
    cap = min(CAP, tok_local, keep_count)
    queries = ref_queries.reshape(item_count, query_count, head_size)
    key_table = cache_keys.reshape(item_count, tok_local, head_size)
    value_table = cache_values.reshape(item_count, tok_local, head_size)
    positions = listed.reshape(item_count, keep_count)

    def swap(x, d):
        return lax.ppermute(x, "ctx", [(j, j ^ d) for j in range(shard_count)])

    me_list = me[None]
    rows = message_rows(items_local, head_size)
    attend = functools.partial(
        partial_attention,
        me_list,
        items=items_local,
        queries=queries,
        key_table=key_table,
        value_table=value_table,
        scale=scale,
    )

    steps = [1 << bit for bit in range(shard_count.bit_length() - 1)]
    if len(steps) > 1:
        steps[:2] = steps[1::-1]
    first, later = steps[0], steps[1:]
    order = [d for d in range(shard_count) if not d & first][::-1]
    half = max(1, len(order) // 2)
    groups = [group for group in (order[:half], order[half:]) if group]

    sent, kept, chain = [], [], ()
    for group in groups:
        part = attend([d ^ first for d in group], dtype=BF16, after=chain)
        sent.append(swap(part, first))
        chain = (part,)
        if not kept:
            listed_here = listed_rows(positions - me * tok_local, key_table, cap)
            pieces = gather_blocks(listed_here, swap, shard_count)
            kept.append(attend(group, dtype=F32, after=chain))
            chain = (kept[0], listed_here)
    kept.append(attend(groups[-1], dtype=F32, after=chain)) if len(groups) > 1 else None
    parts = {
        d: [(kept[g], p), (sent[g], p)]
        for g, group in enumerate(groups)
        for p, d in enumerate(group)
    }
    for step in later:
        for d in sorted((d for d in parts if d & step), reverse=True):
            merged = merge_parts(parts.pop(d), items_local, rows)
            parts[d ^ step].append((swap(merged, step), 0))

    home = positions // tok_local
    earlier = jnp.arange(keep_count)[:, None] < jnp.arange(keep_count)[None, :]
    same = (home[:, :, None] == home[:, None, :]) & earlier[None]
    slots = (home ^ me) * cap + jnp.sum(same.astype(jnp.int32), axis=1)

    weights, inverse = ridge_system(me_list, items_local, slots, queries, pieces, scale)
    solved = solve_items(weights, inverse, parts[0], rows)
    compact_keys = order_rows(slots, pieces, after=(solved,))
    compact_values = place_blocks(me_list, gather_blocks(solved, swap, shard_count))
    shape = (layer_count, head_count, keep_count, head_size)
    return (compact_keys.reshape(shape), compact_values.reshape(shape))


def solution(mesh):
    in_specs = (
        P("grp", "head", "ctx", None),
        P("grp", "head", "ctx", None),
        P("grp", "head", None, None),
        P("grp", "head", None),
    )
    out_specs = (P("grp", "head", None, None), P("grp", "head", None, None))
    return jax.shard_map(shards, mesh=mesh, in_specs=in_specs, out_specs=out_specs, check_vma=False)
```
